128 devices in a mesh: tm: 16 (over x, z_hi, core), freq: 8 (over y, z_lo).
Axes of the slice: x: 4, y: 4, z: 4 (z_hi: 2, z_lo: 2; z = z_hi * 2 + z_lo), core: 2. Of those that a mesh axis runs over, the one named last changes fastest.
Arguments:
- visibility: bfloat16 [2, 32, 1024, 4096], P(None, None, 'freq', 'tm'), may hold values from -6 to 6
- spectrum_power_sum: float32 [1024, 4096], P('freq', 'tm'), may hold values from 50 to 500, as said below
- square_sum: float32 [1024, 4096], P('freq', 'tm'), as said below
- accum_count: int32 [1024, 4096], P('freq', 'tm'), may hold values from 64 to 256
- rfi_mask: int32 [1024, 4096], P('freq', 'tm'), may hold values 0 or 1
- baseline_delay_class: int32 [32, 1], P('freq'), may hold values from 0 to 3
- filter_bank: bfloat16 [4, 1024, 1024], replicated, may hold values from -0.1875 to 0.1875
Outputs:
- filtered: bfloat16 [2, 32, 1024, 4096], P(None, 'freq', None, 'tm')
The draws below stay inside these ranges and needn't reach their ends.
Inputs may be any that keep to these rules, and one draw needn't show every extreme that they name: `spectrum_power_sum`: positive in every sample. `square_sum`: positive in every sample.
All inputs are finite; a program needn't handle non-finite values. No bound on the sum of `rfi_mask` on one device may be relied on, other than what follows from the above.
Results may differ from the reference program's by a relative error of at most 0.0043.
The reference program's roundings to bfloat16 on the way (of `weighted` and `spectrum`) count: a program that leaves them out, or rounds other values in their place, can miss the bound.
Values may be sent and summed in bfloat16 or wider, within the bound.
A program may use at most 128 MiB of HBM per device.

```python
import math
import jax
import jax.numpy as jnp
from jax import lax

RIM = 16
CUTOFF_CLASSES = 4
BASELINE_COUNT = 32
FREQUENCY_COUNT = 1024
SIDEREAL_COUNT = 4096


def flag_fields(key):
    count_key = jax.random.fold_in(key, 101)
    power_key = jax.random.fold_in(key, 202)
    counts = jax.random.randint(count_key, (FREQUENCY_COUNT, SIDEREAL_COUNT), 64, 257).astype(jnp.int32)
    power = jnp.exp(jax.random.uniform(power_key, (FREQUENCY_COUNT, SIDEREAL_COUNT), jnp.float32, math.log(50.0), math.log(500.0)))
    return (counts, power)


def draw_accum_count(key, part):
    counts, power = flag_fields(key)
    return counts


def draw_spectrum_power_sum(key, part):
    counts, power = flag_fields(key)
    return power


def draw_square_sum(key, part):
    counts, power = flag_fields(key)
    ratio_key = jax.random.fold_in(key, 303)
    ratio = jax.random.uniform(ratio_key, (FREQUENCY_COUNT, SIDEREAL_COUNT), jnp.float32, 1.4, 3.2)
    return power * power * ratio / counts.astype(jnp.float32)


def with_ends(values, key, smallest, high):
    longest = values.shape.index(max(values.shape))
    spots = []
    for shift in (0, 1):
        where = [jax.random.randint(jax.random.fold_in(key, axis), (), 0, length) for axis, length in enumerate(values.shape)]
        where[longest] = (where[longest] + shift) % values.shape[longest]
        spots.append(tuple(where))
    return values.at[spots[0]].set(smallest).at[spots[1]].set(high)


def shard_levels(own_key, shape, pieces, low, largest):
    loudness, own = 1.0, jax.random.fold_in(own_key, 6)
    for position, blocks in pieces:
        heights = jnp.exp(jax.random.uniform(jax.random.fold_in(own, position), (blocks,), jnp.float32, low / len(pieces), largest / len(pieces)))
        loudness = loudness * jnp.repeat(heights, shape[position] // blocks).reshape([-1 if axis == position else 1 for axis in range(len(shape))])
    return loudness


def different_ones(own_key, rows, amount, top, lift):
    sequence = jax.random.permutation(jax.random.fold_in(own_key, 1), amount)
    boost = sequence
    for power in range(3):
        boost = boost * boost // amount
    boost = boost * lift // amount
    lots = jax.random.randint(jax.random.fold_in(own_key, 2), (rows, amount), 0, 4096) + boost
    fixed_rows = jax.random.permutation(jax.random.fold_in(own_key, 3), rows)[jnp.arange(amount) % rows]
    lots = jnp.where(jnp.arange(rows)[:, None] == fixed_rows[None, :], 1 << 14, lots)
    score = lots * amount + jnp.arange(amount)
    return lax.top_k(score.astype(jnp.int32), top)[1].astype(jnp.int32)


def noise(own_key, extent, spread, reach, cuts=(), held_as=jnp.bfloat16):
    values = spread * jax.random.normal(own_key, extent, jnp.float32)
    if cuts:
        values = values * shard_levels(own_key, extent, cuts, -0.22, 0.18)
    return jnp.clip(values, -reach, reach).astype(held_as)


def setup_inputs(seed: int = 0) -> dict:
    arg_keys = jax.random.split(jax.random.key(seed), 8)
    return {
        "visibility": noise(arg_keys[0], (2, BASELINE_COUNT, FREQUENCY_COUNT, SIDEREAL_COUNT), 1.0, 6.0, ((2, 8), (3, 16))),
        "spectrum_power_sum": draw_spectrum_power_sum(jax.random.fold_in(arg_keys[7], 71), 0),
        "square_sum": draw_square_sum(jax.random.fold_in(arg_keys[7], 71), 0),
        "accum_count": draw_accum_count(jax.random.fold_in(arg_keys[7], 71), 0),
        "rfi_mask": with_ends((jax.random.randint(arg_keys[4], (FREQUENCY_COUNT, SIDEREAL_COUNT), 0, 10) < 9).astype(jnp.int32), jax.random.fold_in(arg_keys[4], 1), 0, 1),
        "baseline_delay_class": different_ones(arg_keys[5], BASELINE_COUNT, CUTOFF_CLASSES, 1, 2048),
        "filter_bank": noise(arg_keys[6], (CUTOFF_CLASSES, FREQUENCY_COUNT, FREQUENCY_COUNT), FREQUENCY_COUNT ** -0.5, 0.1875),
    }


def smooth_periodic(flag_weight):
    total = jnp.zeros(flag_weight.shape, jnp.float32)
    for offset in range(2 * RIM + 1):
        factor = (RIM + 1 - abs(offset - RIM)) / float((RIM + 1) ** 2)
        total = total + factor * jnp.roll(flag_weight, RIM - offset, axis=1)
    return total

def reference(visibility, spectrum_power_sum, square_sum, accum_count, rfi_mask, baseline_delay_class, filter_bank):
    counts = accum_count.astype(jnp.float32)
    kurtosis = (counts + 1.0) / (counts - 1.0) * (counts * square_sum / (spectrum_power_sum * spectrum_power_sum) - 1.0)
    flag_weight = rfi_mask.astype(jnp.float32) * jnp.exp(-2.0 * (kurtosis - 1.0) ** 2)
    smooth_weight = smooth_periodic(flag_weight)
    norm_scale = 1.0 / math.sqrt(SIDEREAL_COUNT)

    def per_baseline(inputs):
        vis_one, class_one = inputs
        weighted = (vis_one.astype(jnp.float32) * smooth_weight[None]).astype(jnp.bfloat16)
        widened = weighted.astype(jnp.float32)
        transformed = jnp.fft.fft(widened[0] + 1j * widened[1], axis=-1) * norm_scale
        spectrum = jnp.stack([jnp.real(transformed), jnp.imag(transformed)]).astype(jnp.bfloat16)
        matrix = lax.dynamic_index_in_dim(filter_bank, class_one[0].astype(jnp.int32), 0, keepdims=False)
        first = jnp.dot(matrix, spectrum[0], preferred_element_type=jnp.float32)
        second = jnp.dot(matrix, spectrum[1], preferred_element_type=jnp.float32)
        return jnp.stack([first, second]).astype(jnp.bfloat16)
    result = lax.map(per_baseline, (jnp.moveaxis(visibility, 1, 0), baseline_delay_class))
    return jnp.moveaxis(result, 0, 1)
```

```python
import functools
import math
import random

import jax
import jax.numpy as jnp
import numpy as np
from jax import lax
from jax.experimental import pallas as pl
from jax.experimental.pallas import tpu as pltpu
from jax.sharding import PartitionSpec as P

RIM = 16
MESH = pl.DeviceIdType.MESH
TM, FREQ = 16, 8
CHAN, LEN = 128, 256
SAMPLES = TM * LEN
BLOCK = 4
BF, F32 = jnp.bfloat16, jnp.float32
OFFSETS = [(a, b, c) for a in range(4) for b in range(2) for c in range(2)]


def shuffled(seed):
    order = list(OFFSETS)
    random.Random(seed).shuffle(order)
    return order


def dft_tables():
    k = np.arange(LEN)
    angle = 2.0 * np.pi / LEN * (k[:, None] * k[None, :] % LEN)
    c, s = np.cos(angle), np.sin(angle)
    full = np.block([[c, s], [-s, c]]).astype(np.float32)
    high = full.astype(jnp.bfloat16)
    low = (full - high.astype(np.float32)).astype(jnp.bfloat16)
    turn = 2.0 * np.pi / SAMPLES * (np.arange(TM)[:, None] * k[None, :])
    twist = np.stack([np.cos(turn), np.sin(turn)]) / math.sqrt(SAMPLES)
    return high, low, twist.astype(np.float32)


def order_table():
    m = np.arange(LEN)
    table = np.zeros((LEN, LEN), np.float32)
    table[m, (m % TM) * TM + m // TM] = 1.0
    return table.astype(jnp.bfloat16)


def place(i, j):
    return i // 4, lax.rem(i // 2, 2), lax.rem(i, 2), j // 2, lax.rem(j, 2)


def tm_index(x, zh, core, o):
    return lax.rem(x + o[0], 4) * 4 + lax.rem(zh + o[1], 2) * 2 + lax.rem(core + o[2], 2)


def owner_block(x, core, y, zl, e):
    return lax.rem(y + 2 * core + lax.rem(e + x, 2), 4) * 2 + lax.rem(zl + e, 2)


def cmul_w16(r, i, n):
    n %= 16
    if n == 0:
        return r, i
    if n == 4:
        return i, -r
    if n == 8:
        return -r, -i
    if n == 12:
        return -i, r
    if n == 2:
        h = math.sqrt(0.5)
        return (r + i) * h, (i - r) * h
    if n == 6:
        h = math.sqrt(0.5)
        return (i - r) * h, -(r + i) * h
    c, s = math.cos(2 * math.pi * n / 16), math.sin(2 * math.pi * n / 16)
    return r * c + i * s, i * c - r * s


def radix4(v):
    (ar, ai), (br, bi), (cr, ci), (dr, di) = v
    pr, pi = ar + cr, ai + ci
    qr, qi = ar - cr, ai - ci
    sr, si = br + dr, bi + di
    tr, ti = br - dr, bi - di
    return [(pr + sr, pi + si), (qr + ti, qi - tr), (pr - sr, pi - si), (qr - ti, qi + tr)]


def exchange_kernel(
    vis_hbm, power_ref, square_ref, count_ref, mask_ref, high_ref, low_ref, twist_ref,
    out_ref,
    vis, pad, smooth, recv, yhigh, ylow, send,
    vis_sem, halo_send, halo_recv, send1, recv1, send2, recv2,
):
    i, j = lax.axis_index("tm"), lax.axis_index("freq")
    x, zh, core, y, zl = place(i, j)
    barrier = pltpu.get_barrier_semaphore()

    def greet(k, _):
        n = lax.rem(i * FREQ + j + k, TM * FREQ)
        pl.semaphore_signal(barrier, inc=1, device_id=(n // FREQ, lax.rem(n, FREQ)), device_id_type=MESH)
        return 0

    lax.fori_loop(1, TM * FREQ, greet, 0)
    load = pltpu.make_async_copy(vis_hbm, vis, vis_sem)
    load.start()

    counts = count_ref[...].astype(F32)
    power = power_ref[...]
    kurtosis = (counts + 1.0) / (counts - 1.0) * (counts * square_ref[...] / (power * power) - 1.0)
    pad[:, 128:384] = mask_ref[...].astype(F32) * jnp.exp(-2.0 * (kurtosis - 1.0) ** 2)

    pl.semaphore_wait(barrier, TM * FREQ - 1)
    right, left = lax.rem(i + 1, TM), lax.rem(i + TM - 1, TM)
    to_right = pltpu.make_async_remote_copy(
        pad.at[:, 256:384], pad.at[:, 0:128], halo_send.at[0], halo_recv.at[0],
        device_id=(right, j), device_id_type=MESH)
    to_left = pltpu.make_async_remote_copy(
        pad.at[:, 128:256], pad.at[:, 384:512], halo_send.at[1], halo_recv.at[1],
        device_id=(left, j), device_id_type=MESH)
    to_right.start()
    to_left.start()
    to_right.wait()
    to_left.wait()

    width = 512
    for rows in range(0, CHAN, 32):
        base = pad[rows : rows + 32, :]
        for direction in (0, 1):
            def shift(v, n):
                return pltpu.roll(v, n if direction else width - n, 1)
            total = base
            for n in (1, 2, 4, 8):
                total = total + shift(total, n)
            base = total + shift(base, 16)
        smooth[rows : rows + 32, :] = base[:, 128:384] * (1.0 / (RIM + 1) ** 2)

    load.wait()

    def weigh(e, o):
        d = tm_index(x, zh, core, o)
        dx, dzh, dcore, _, _ = place(d, j)
        b = BLOCK * owner_block(dx, dcore, y, zl, e) + 2 * (dx // 2) + dzh
        for c in range(2):
            vis[c, b] = (vis[c, b].astype(F32) * smooth[...]).astype(BF)
            if o == (0, 0, 0):
                pltpu.make_async_copy(vis.at[c, b], recv.at[e, i, c], recv1.at[e]).start()
            else:
                pltpu.make_async_remote_copy(
                    vis.at[c, b], recv.at[e, i, c], send1.at[e], recv1.at[e],
                    device_id=(d, j), device_id_type=MESH).start()

    for e in range(2):
        for o in shuffled(11 + e):
            weigh(e, o)

    for e in range(2):
        pltpu.make_async_copy(recv.at[e], recv.at[e], recv1.at[e]).wait()

        def combine(step, _):
            rows = pl.ds(pl.multiple_of((step // 2) * 16, 16), 16)
            col = pl.multiple_of(lax.rem(step, 2) * 128, 128)
            cols = pl.ds(col, 128)
            inner = []
            for b in range(4):
                part = []
                for a in range(4):
                    p = 4 * a + b
                    part.append((recv[e, p, 0, rows, cols].astype(F32), recv[e, p, 1, rows, cols].astype(F32)))
                part = radix4(part)
                inner.append([cmul_w16(*part[c], b * c) for c in range(4)])
            for c in range(4):
                outer = radix4([inner[b][c] for b in range(4)])
                for d in range(4):
                    q = c + 4 * d
                    r, m = outer[d]
                    cosine = twist_ref[0, q : q + 1, cols]
                    sine = twist_ref[1, q : q + 1, cols]
                    for part, value in ((0, r * cosine + m * sine), (1, m * cosine - r * sine)):
                        top = value.astype(BF)
                        at = (q, rows, pl.ds(pl.multiple_of(col + LEN * part, 128), 128))
                        yhigh[at] = top
                        ylow[at] = (value - top.astype(F32)).astype(BF)
            return 0

        lax.fori_loop(0, 2 * CHAN // 16, combine, 0)

        dims = (((1,), (1,)), ((), ()))

        def transform(step, _):
            q = 2 * step
            yh = yhigh[pl.ds(q, 2)].reshape(2 * CHAN, 2 * LEN)
            yl = ylow[pl.ds(q, 2)].reshape(2 * CHAN, 2 * LEN)
            for part in range(2):
                rows = slice(LEN * part, LEN * part + LEN)
                value = lax.dot_general(high_ref[rows], yh, dims, preferred_element_type=F32)
                value += lax.dot_general(high_ref[rows], yl, dims, preferred_element_type=F32)
                value += lax.dot_general(low_ref[rows], yh, dims, preferred_element_type=F32)
                value = value.astype(BF)
                for h in range(2):
                    at = pl.ds(pl.multiple_of((q + h) * 16, 16), 16)
                    send[e, part, :, at, :] = value[:, CHAN * h : CHAN * h + CHAN].reshape(TM, TM, CHAN)
            return 0

        lax.fori_loop(0, TM // 2, transform, 0)

        dest = owner_block(x, core, y, zl, e)
        slot = 2 * (x // 2) + zh
        lanes = pl.ds(pl.multiple_of(j * CHAN, CHAN), CHAN)
        for o in shuffled(21 + e):
            d = tm_index(x, zh, core, o)
            for c in range(2):
                def away():
                    pltpu.make_async_remote_copy(
                        send.at[e, c, d], out_ref.at[slot, c, :, lanes], send2, recv2,
                        device_id=(d, dest), device_id_type=MESH).start()
                if o != (0, 0, 0) or e == 1:
                    away()
                else:
                    pl.when(dest != j)(away)

                    @pl.when(dest == j)
                    def _():
                        pltpu.make_async_copy(send.at[e, c, d], out_ref.at[slot, c, :, lanes], recv2).start()

    pltpu.make_async_copy(out_ref, out_ref, recv2).wait()
    for e in range(2):
        pltpu.make_async_copy(recv.at[e, pl.ds(0, TM - 1)], recv.at[e, pl.ds(0, TM - 1)], send1.at[e]).wait()
    own = owner_block(x, core, y, zl, 0) == j

    @pl.when(own)
    def _():
        whole = vis.at[:, pl.ds(0, 31)]
        pltpu.make_async_copy(whole, whole, send2).wait()

    @pl.when(jnp.logical_not(own))
    def _():
        pltpu.make_async_copy(vis, vis, send2).wait()


def exchange(vis, power, square, count, mask):
    high, low, twist = dft_tables()
    vmem, hbm = pl.BlockSpec(memory_space=pltpu.VMEM), pl.BlockSpec(memory_space=pl.ANY)
    dma = pltpu.SemaphoreType.DMA
    return pl.pallas_call(
        exchange_kernel,
        name="exchange",
        out_shape=jax.ShapeDtypeStruct((BLOCK, 2, LEN, FREQ * CHAN), BF),
        in_specs=[hbm] + [vmem] * 7,
        out_specs=hbm,
        scratch_shapes=[
            pltpu.VMEM((2, BLOCK * FREQ, CHAN, LEN), BF),
            pltpu.VMEM((CHAN, 512), F32),
            pltpu.VMEM((CHAN, LEN), F32),
            pltpu.VMEM((2, TM, 2, CHAN, LEN), BF),
            pltpu.VMEM((TM, CHAN, 2 * LEN), BF),
            pltpu.VMEM((TM, CHAN, 2 * LEN), BF),
            pltpu.VMEM((2, 2, TM, LEN, CHAN), BF),
            dma, dma((2,)), dma((2,)), dma((2,)), dma((2,)), dma, dma,
        ],
        compiler_params=pltpu.CompilerParams(
            collective_id=0, has_side_effects=True, vmem_limit_bytes=56 << 20),
    )(vis, power, square, count, mask, jnp.asarray(high), jnp.asarray(low), jnp.asarray(twist))


def filter_kernel(class_ref, spec_ref, order_ref, bank_ref, out_ref, held):
    @pl.when(pl.program_id(1) == 0)
    def _():
        for c in range(2):
            held[LEN * c : LEN * c + LEN, :] = jnp.dot(
                order_ref[...], spec_ref[0, c], preferred_element_type=F32).astype(BF)

    value = lax.dot_general(
        bank_ref[0], held[...], (((1,), (1,)), ((), ())), preferred_element_type=F32).astype(BF)
    for c in range(2):
        out_ref[c, 0] = value[:, LEN * c : LEN * c + LEN]


def delay_filter(spectrum, classes, bank):
    width = FREQ * CHAN
    tile = 512
    return pl.pallas_call(
        filter_kernel,
        name="delay_filter",
        out_shape=jax.ShapeDtypeStruct((2, BLOCK, width, LEN), BF),
        grid_spec=pltpu.PrefetchScalarGridSpec(
            num_scalar_prefetch=1,
            grid=(BLOCK, width // tile),
            in_specs=[
                pl.BlockSpec((1, 2, LEN, width), lambda b, g, cls: (b, 0, 0, 0)),
                pl.BlockSpec((LEN, LEN), lambda b, g, cls: (0, 0)),
                pl.BlockSpec((1, tile, width), lambda b, g, cls: (cls[b], g, 0)),
            ],
            out_specs=pl.BlockSpec((2, 1, tile, LEN), lambda b, g, cls: (0, b, g, 0)),
            scratch_shapes=[pltpu.VMEM((2 * LEN, width), BF)],
        ),
        compiler_params=pltpu.CompilerParams(vmem_limit_bytes=40 << 20),
    )(classes, spectrum, jnp.asarray(order_table()), bank)


def shards(visibility, power, square, count, mask, classes, bank):
    spectrum = exchange(visibility, power, square, count, mask)
    return delay_filter(spectrum, classes[:, 0], bank)


def solution(mesh):
    in_specs = (
        P(None, None, "freq", "tm"),
        P("freq", "tm"),
        P("freq", "tm"),
        P("freq", "tm"),
        P("freq", "tm"),
        P("freq", None),
        P(),
    )
    out_specs = P(None, "freq", None, "tm")
    return jax.shard_map(shards, mesh=mesh, in_specs=in_specs, out_specs=out_specs, check_vma=False)
```

```python
import functools
import math
import random

import jax
import jax.numpy as jnp
import numpy as np
from jax import lax
from jax.experimental import pallas as pl
from jax.experimental.pallas import tpu as pltpu
from jax.sharding import PartitionSpec as P

RIM = 16
MESH = pl.DeviceIdType.MESH
TM, FREQ = 16, 8
CHAN, LEN = 128, 256
SAMPLES = TM * LEN
BLOCK = 4
BF, F32 = jnp.bfloat16, jnp.float32
PIECES_1, PIECES_2 = 4, 4
ORDER_1, ORDER_2 = 11, 21
OFFSETS = [(a, b, c) for a in range(4) for b in range(2) for c in range(2)]


def shuffled(seed):
    order = list(OFFSETS)
    random.Random(seed).shuffle(order)
    return order


def dft_tables():
    k = np.arange(LEN)
    angle = 2.0 * np.pi / LEN * (k[:, None] * k[None, :] % LEN)
    c, s = np.cos(angle), np.sin(angle)
    full = np.block([[c, s], [-s, c]]).astype(np.float32)
    high = full.astype(jnp.bfloat16)
    low = (full - high.astype(np.float32)).astype(jnp.bfloat16)
    turn = 2.0 * np.pi / SAMPLES * (np.arange(TM)[:, None] * k[None, :])
    twist = np.stack([np.cos(turn), np.sin(turn)]) / math.sqrt(SAMPLES)
    return high, low, twist.astype(np.float32)


def order_table():
    m = np.arange(LEN)
    table = np.zeros((LEN, LEN), np.float32)
    table[m, (m % TM) * TM + m // TM] = 1.0
    return table.astype(jnp.bfloat16)


def place(i, j):
    return i // 4, lax.rem(i // 2, 2), lax.rem(i, 2), j // 2, lax.rem(j, 2)


def tm_index(x, zh, core, o):
    return lax.rem(x + o[0], 4) * 4 + lax.rem(zh + o[1], 2) * 2 + lax.rem(core + o[2], 2)


def owner_block(x, core, y, zl, e):
    return lax.rem(y + 2 * core + lax.rem(e + x, 2), 4) * 2 + lax.rem(zl + x // 2, 2)


def cmul_w16(r, i, n):
    n %= 16
    if n == 0:
        return r, i
    if n == 4:
        return i, -r
    if n == 8:
        return -r, -i
    if n == 12:
        return -i, r
    if n == 2:
        h = math.sqrt(0.5)
        return (r + i) * h, (i - r) * h
    if n == 6:
        h = math.sqrt(0.5)
        return (i - r) * h, -(r + i) * h
    c, s = math.cos(2 * math.pi * n / 16), math.sin(2 * math.pi * n / 16)
    return r * c + i * s, i * c - r * s


def radix4(v):
    (ar, ai), (br, bi), (cr, ci), (dr, di) = v
    pr, pi = ar + cr, ai + ci
    qr, qi = ar - cr, ai - ci
    sr, si = br + dr, bi + di
    tr, ti = br - dr, bi - di
    return [(pr + sr, pi + si), (qr + ti, qi - tr), (pr - sr, pi - si), (qr - ti, qi + tr)]


def box(v, direction):
    width = v.shape[1]

    def shift(u, n):
        return pltpu.roll(u, n if direction else width - n, 1)

    total = v
    for n in (1, 2, 4, 8):
        total = total + shift(total, n)
    return total + shift(v, 16)


def triangle(v):
    return box(box(v, 0), 1) * (1.0 / (RIM + 1) ** 2)


def exchange_kernel(
    class_ref, vis_hbm, power_ref, square_ref, count_ref, mask_ref, high_ref, low_ref, twist_ref, order_ref, bank_hbm,
    last_ref, real_ref, imag_ref,
    vis, flags, edge, smooth, recv, yhigh, ylow, send, spec, bank, held, done,
    load_sem, halo_send, halo_recv, send1, recv1, send2, recv2, done_sem,
):
    i, j = lax.axis_index("tm"), lax.axis_index("freq")
    x, zh, core, y, zl = place(i, j)
    barrier = pltpu.get_barrier_semaphore()

    for k in range(1, TM):
        pl.semaphore_signal(barrier, inc=1, device_id=(lax.rem(i + k, TM), j), device_id_type=MESH)
    for k in range(1, FREQ):
        pl.semaphore_signal(barrier, inc=1, device_id=(i, lax.rem(j + k, FREQ)), device_id_type=MESH)
    load = pltpu.make_async_copy(vis_hbm, vis, load_sem.at[0])
    load.start()

    counts = count_ref[...].astype(F32)
    power = power_ref[...]
    kurtosis = (counts + 1.0) / (counts - 1.0) * (counts * square_ref[...] / (power * power) - 1.0)
    flags[...] = mask_ref[...].astype(F32) * jnp.exp(-2.0 * (kurtosis - 1.0) ** 2)

    pl.semaphore_wait(barrier, TM + FREQ - 2)
    right, left = lax.rem(i + 1, TM), lax.rem(i + TM - 1, TM)
    to_right = pltpu.make_async_remote_copy(
        flags.at[:, LEN - 128 : LEN], edge.at[0], halo_send.at[0], halo_recv.at[0],
        device_id=(right, j), device_id_type=MESH)
    to_left = pltpu.make_async_remote_copy(
        flags.at[:, 0:128], edge.at[1], halo_send.at[1], halo_recv.at[1],
        device_id=(left, j), device_id_type=MESH)
    to_right.start()
    to_left.start()
    blank = jnp.zeros((32, 128), F32)
    for rows in range(0, CHAN, 32):
        own = jnp.concatenate([blank, flags[rows : rows + 32, :], blank], axis=1)
        smooth[rows : rows + 32, :] = triangle(own)[:, 128 : 128 + LEN]
    to_right.wait()
    to_left.wait()
    lane = lax.broadcasted_iota(jnp.int32, (CHAN, 128), 1)
    first_lanes, last_lanes = lane < RIM, lane >= 128 - RIM
    before = triangle(jnp.where(last_lanes, edge[0], 0.0))
    after = triangle(jnp.where(first_lanes, edge[1], 0.0))
    smooth[:, 0:128] += jnp.where(first_lanes, before, 0.0)
    smooth[:, LEN - 128 : LEN] += jnp.where(last_lanes, after, 0.0)

    load.wait()
    bank_load = pltpu.make_async_copy(bank_hbm, bank, load_sem.at[1])
    bank_load.start()

    def first(e, o):
        d = tm_index(x, zh, core, o)
        dx, dzh, dcore, _, _ = place(d, j)
        return d, BLOCK * owner_block(dx, dcore, y, zl, e) + 2 * e + dzh

    def weigh(e, o):
        d, b = first(e, o)
        for c in range(2):
            value = (vis[c, b].astype(F32) * smooth[...]).astype(BF)
            if o == (0, 0, 0):
                recv[e, i, c] = value
            else:
                vis[c, b] = value

    def hand(e, o, c, rows):
        d, b = first(e, o)
        pltpu.make_async_remote_copy(
            vis.at[c, b, rows], recv.at[e, i, c, rows], send1.at[e], recv1.at[e],
            device_id=(d, j), device_id_type=MESH).start()

    size = CHAN // PIECES_1
    for e in range(2):
        order = shuffled(ORDER_1 + e)
        remote = [o for o in order if o != (0, 0, 0)]
        for o in order:
            weigh(e, o)
            if o != (0, 0, 0):
                hand(e, o, 0, pl.ds(0, size))
        def rest(q, _):
            rows = pl.ds(pl.multiple_of(q * size, size), size)
            for o in remote:
                hand(e, o, 0, rows)
            return 0
        lax.fori_loop(1, PIECES_1, rest, 0)
        def rest(q, _):
            rows = pl.ds(pl.multiple_of(q * size, size), size)
            for o in remote:
                hand(e, o, 1, rows)
            return 0
        lax.fori_loop(0, PIECES_1, rest, 0)

    for e in range(2):
        others = recv.at[e, pl.ds(0, TM - 1)]
        pltpu.make_async_copy(others, others, recv1.at[e]).wait()

        def combine(step, _):
            rows = pl.ds(pl.multiple_of((step // 2) * 16, 16), 16)
            col = pl.multiple_of(lax.rem(step, 2) * 128, 128)
            cols = pl.ds(col, 128)
            inner = []
            for b in range(4):
                part = []
                for a in range(4):
                    p = 4 * a + b
                    part.append((recv[e, p, 0, rows, cols].astype(F32), recv[e, p, 1, rows, cols].astype(F32)))
                part = radix4(part)
                inner.append([cmul_w16(*part[c], b * c) for c in range(4)])
            for c in range(4):
                outer = radix4([inner[b][c] for b in range(4)])
                for d in range(4):
                    q = c + 4 * d
                    r, m = outer[d]
                    cosine = twist_ref[0, q : q + 1, cols]
                    sine = twist_ref[1, q : q + 1, cols]
                    for part, value in ((0, r * cosine + m * sine), (1, m * cosine - r * sine)):
                        top = value.astype(BF)
                        at = (q, rows, pl.ds(pl.multiple_of(col + LEN * part, 128), 128))
                        yhigh[at] = top
                        ylow[at] = (value - top.astype(F32)).astype(BF)
            return 0

        lax.fori_loop(0, 2 * CHAN // 16, combine, 0)

        dims = (((1,), (1,)), ((), ()))

        def transform(step, _):
            q = 2 * step
            yh = yhigh[pl.ds(q, 2)].reshape(2 * CHAN, 2 * LEN)
            yl = ylow[pl.ds(q, 2)].reshape(2 * CHAN, 2 * LEN)
            for part in range(2):
                rows = slice(LEN * part, LEN * part + LEN)
                value = lax.dot_general(high_ref[rows], yh, dims, preferred_element_type=F32)
                value += lax.dot_general(high_ref[rows], yl, dims, preferred_element_type=F32)
                value += lax.dot_general(low_ref[rows], yh, dims, preferred_element_type=F32)
                value = value.astype(BF)
                for h in range(2):
                    at = pl.ds(pl.multiple_of((q + h) * 16, 16), 16)
                    send[e, part, :, at, :] = value[:, CHAN * h : CHAN * h + CHAN].reshape(TM, TM, CHAN)
            return 0

        lax.fori_loop(0, TM // 2, transform, 0)

        dest = owner_block(x, core, y, zl, e)
        lanes = pl.ds(pl.multiple_of(j * CHAN, CHAN), CHAN)
        size2 = LEN // PIECES_2
        for c in range(2):
            part = 2 * e + c
            target = last_ref if part == 3 else spec.at[part]

            def share(q, _):
                rows = pl.ds(pl.multiple_of(q * size2, size2), size2)
                for o in shuffled(ORDER_2 + e):
                    d = tm_index(x, zh, core, o)

                    def away():
                        pltpu.make_async_remote_copy(
                            send.at[e, c, d, rows], target.at[zh, rows, lanes], send2, recv2.at[part],
                            device_id=(d, dest), device_id_type=MESH).start()

                    if o != (0, 0, 0):
                        away()
                    else:
                        pl.when(dest != j)(away)

                        @pl.when(dest == j)
                        def _():
                            pltpu.make_async_copy(
                                send.at[e, c, d, rows], target.at[zh, rows, lanes], recv2.at[part]).start()
                return 0

            lax.fori_loop(0, PIECES_2, share, 0)

    bank_load.wait()
    out = []
    for part in range(3):
        e, c = part // 2, part % 2
        pltpu.make_async_copy(spec.at[part], spec.at[part], recv2.at[part]).wait()
        for z in range(2):
            held[...] = jnp.dot(order_ref[...], spec[part, z], preferred_element_type=F32).astype(BF)

            def rows_of(g, _):
                at = pl.ds(pl.multiple_of(g * 512, 512), 512)
                done[part, z, at, :] = lax.dot_general(
                    bank[class_ref[2 * e + z], at, :], held[...], (((1,), (1,)), ((), ())),
                    preferred_element_type=F32).astype(BF)
                return 0

            lax.fori_loop(0, 2, rows_of, 0)
        out.append(pltpu.make_async_copy(
            done.at[part], imag_ref if c else real_ref.at[pl.ds(2 * e, 2)], done_sem.at[part]))
        out[-1].start()

    pltpu.make_async_copy(last_ref, last_ref, recv2.at[3]).wait()
    for copy in out:
        copy.wait()
    for e in range(2):
        others = recv.at[e, pl.ds(0, TM - 1)]
        pltpu.make_async_copy(others, others, send1.at[e]).wait()
    own = jnp.logical_or(owner_block(x, core, y, zl, 0) == j, owner_block(x, core, y, zl, 1) == j)

    @pl.when(own)
    def _():
        most = vis.at[:, pl.ds(0, BLOCK * FREQ - 1)]
        pltpu.make_async_copy(most, most, send2).wait()

    @pl.when(jnp.logical_not(own))
    def _():
        pltpu.make_async_copy(vis, vis, send2).wait()


def exchange(classes, vis, power, square, count, mask, bank):
    high, low, twist = dft_tables()
    vmem, hbm = pl.BlockSpec(memory_space=pltpu.VMEM), pl.BlockSpec(memory_space=pl.ANY)
    dma = pltpu.SemaphoreType.DMA
    width = FREQ * CHAN
    return pl.pallas_call(
        exchange_kernel,
        name="exchange",
        out_shape=(
            jax.ShapeDtypeStruct((2, LEN, width), BF),
            jax.ShapeDtypeStruct((BLOCK, width, LEN), BF),
            jax.ShapeDtypeStruct((2, width, LEN), BF),
        ),
        in_specs=[pl.BlockSpec(memory_space=pltpu.SMEM), hbm] + [vmem] * 8 + [hbm],
        out_specs=(hbm, hbm, hbm),
        scratch_shapes=[
            pltpu.VMEM((2, BLOCK * FREQ, CHAN, LEN), BF),
            pltpu.VMEM((CHAN, LEN), F32),
            pltpu.VMEM((2, CHAN, 128), F32),
            pltpu.VMEM((CHAN, LEN), F32),
            pltpu.VMEM((2, TM, 2, CHAN, LEN), BF),
            pltpu.VMEM((TM, CHAN, 2 * LEN), BF),
            pltpu.VMEM((TM, CHAN, 2 * LEN), BF),
            pltpu.VMEM((2, 2, TM, LEN, CHAN), BF),
            pltpu.VMEM((3, 2, LEN, width), BF),
            pltpu.VMEM((4, width, width), BF),
            pltpu.VMEM((LEN, width), BF),
            pltpu.VMEM((3, 2, width, LEN), BF),
            dma((2,)), dma((2,)), dma((2,)), dma((2,)), dma((2,)), dma, dma((4,)), dma((3,)),
        ],
        compiler_params=pltpu.CompilerParams(
            collective_id=0, has_side_effects=True, vmem_limit_bytes=56 << 20),
    )(classes, vis, power, square, count, mask, jnp.asarray(high), jnp.asarray(low), jnp.asarray(twist),
      jnp.asarray(order_table()), bank)


def finish_kernel(class_ref, last_ref, order_ref, bank_hbm, real_hbm, imag_hbm, out_ref, bank, held, done, kept,
                  bank_sem, kept_sem, copy_sem, done_sem):
    loads = []
    for z in range(2):
        for h in range(2):
            rows = pl.ds(512 * h, 512)
            loads.append(pltpu.make_async_copy(
                bank_hbm.at[class_ref[2 + z], rows], bank.at[z, rows], bank_sem.at[z, h]))
            loads[-1].start()
    early = []
    for n in range(BLOCK + 2):
        source = real_hbm.at[n] if n < BLOCK else imag_hbm.at[n - BLOCK]
        early.append(pltpu.make_async_copy(source, kept.at[n], kept_sem.at[n]))
        early[-1].start()
    copies = []
    for z in range(2):
        held[z] = jnp.dot(order_ref[...], last_ref[z], preferred_element_type=F32).astype(BF)
    for n in range(BLOCK + 2):
        early[n].wait()
        copies.append(pltpu.make_async_copy(kept.at[n], out_ref.at[n // BLOCK, n % BLOCK], copy_sem.at[n]))
        copies[-1].start()
    for z in range(2):
        for h in range(2):
            loads[2 * z + h].wait()
            rows = pl.ds(512 * h, 512)
            done[z, rows, :] = lax.dot_general(
                bank[z, rows, :], held[z], (((1,), (1,)), ((), ())), preferred_element_type=F32).astype(BF)
            copies.append(pltpu.make_async_copy(done.at[z, rows], out_ref.at[1, 2 + z, rows], done_sem.at[z, h]))
            copies[-1].start()
    for copy in copies:
        copy.wait()


def finish(classes, last, bank, real, imag):
    width = FREQ * CHAN
    vmem, hbm = pl.BlockSpec(memory_space=pltpu.VMEM), pl.BlockSpec(memory_space=pl.ANY)
    dma = pltpu.SemaphoreType.DMA
    return pl.pallas_call(
        finish_kernel,
        name="finish",
        out_shape=jax.ShapeDtypeStruct((2, BLOCK, width, LEN), BF),
        in_specs=[pl.BlockSpec(memory_space=pltpu.SMEM), vmem, vmem, hbm, hbm, hbm],
        out_specs=hbm,
        scratch_shapes=[
            pltpu.VMEM((2, width, width), BF),
            pltpu.VMEM((2, LEN, width), BF),
            pltpu.VMEM((2, width, LEN), BF),
            pltpu.VMEM((BLOCK + 2, width, LEN), BF),
            dma((2, 2)), dma((BLOCK + 2,)), dma((BLOCK + 2,)), dma((2, 2)),
        ],
        compiler_params=pltpu.CompilerParams(vmem_limit_bytes=60 << 20),
    )(classes, last, jnp.asarray(order_table()), bank, real, imag)


def shards(visibility, power, square, count, mask, classes, bank):
    classes = classes[:, 0]
    last, real, imag = exchange(classes, visibility, power, square, count, mask, bank)
    return finish(classes, last, bank, real, imag)


def solution(mesh):
    in_specs = (
        P(None, None, "freq", "tm"),
        P("freq", "tm"),
        P("freq", "tm"),
        P("freq", "tm"),
        P("freq", "tm"),
        P("freq", None),
        P(),
    )
    out_specs = P(None, "freq", None, "tm")
    return jax.shard_map(shards, mesh=mesh, in_specs=in_specs, out_specs=out_specs, check_vma=False)
```

```python
import functools
import math
import random

import jax
import jax.numpy as jnp
import numpy as np
from jax import lax
from jax.experimental import pallas as pl
from jax.experimental.pallas import tpu as pltpu
from jax.sharding import PartitionSpec as P

RIM = 16
MESH = pl.DeviceIdType.MESH
TM, FREQ = 16, 8
CHAN, LEN = 128, 256
SAMPLES = TM * LEN
BLOCK = 4
BF, F32 = jnp.bfloat16, jnp.float32
PIECES_1, PIECES_2 = 4, 8
ORDER_1, ORDER_2 = 11, 21
OFFSETS = [(a, b, c) for a in range(4) for b in range(2) for c in range(2)]


def shuffled(seed):
    order = list(OFFSETS)
    random.Random(seed).shuffle(order)
    return order


def dft_tables():
    k = np.arange(LEN)
    angle = 2.0 * np.pi / LEN * (k[:, None] * k[None, :] % LEN)
    c, s = np.cos(angle), np.sin(angle)
    full = np.block([[c, s], [-s, c]]).astype(np.float32)
    high = full.astype(jnp.bfloat16)
    low = (full - high.astype(np.float32)).astype(jnp.bfloat16)
    turn = 2.0 * np.pi / SAMPLES * (np.arange(TM)[:, None] * k[None, :])
    twist = np.stack([np.cos(turn), np.sin(turn)]) / math.sqrt(SAMPLES)
    return high, low, twist.astype(np.float32)


def row_order():
    m = lax.broadcasted_iota(jnp.int32, (LEN, LEN), 0)
    r = lax.broadcasted_iota(jnp.int32, (LEN, LEN), 1)
    return jnp.where(lax.rem(m, TM) * TM + m // TM == r, 1.0, 0.0).astype(BF)


def place(i, j):
    return i // 4, lax.rem(i // 2, 2), lax.rem(i, 2), j // 2, lax.rem(j, 2)


def tm_index(x, zh, core, o):
    return lax.rem(x + o[0], 4) * 4 + lax.rem(zh + o[1], 2) * 2 + lax.rem(core + o[2], 2)


def owner_block(x, core, y, zl, e):
    return lax.rem(y + 2 * core + lax.rem(e + x, 2), 4) * 2 + lax.rem(zl + x // 2, 2)


def cmul_w16(r, i, n):
    n %= 16
    if n == 0:
        return r, i
    if n == 4:
        return i, -r
    if n == 8:
        return -r, -i
    if n == 12:
        return -i, r
    if n == 2:
        h = math.sqrt(0.5)
        return (r + i) * h, (i - r) * h
    if n == 6:
        h = math.sqrt(0.5)
        return (i - r) * h, -(r + i) * h
    c, s = math.cos(2 * math.pi * n / 16), math.sin(2 * math.pi * n / 16)
    return r * c + i * s, i * c - r * s


def radix4(v):
    (ar, ai), (br, bi), (cr, ci), (dr, di) = v
    pr, pi = ar + cr, ai + ci
    qr, qi = ar - cr, ai - ci
    sr, si = br + dr, bi + di
    tr, ti = br - dr, bi - di
    return [(pr + sr, pi + si), (qr + ti, qi - tr), (pr - sr, pi - si), (qr - ti, qi + tr)]


def box(v, direction):
    width = v.shape[1]

    def shift(u, n):
        return pltpu.roll(u, n if direction else width - n, 1)

    total = v
    for n in (1, 2, 4, 8):
        total = total + shift(total, n)
    return total + shift(v, 16)


def triangle(v):
    return box(box(v, 0), 1) * (1.0 / (RIM + 1) ** 2)


def exchange_kernel(
    class_ref, vis_hbm, power_hbm, square_hbm, count_hbm, mask_hbm, high_hbm, low_hbm, twist_hbm, bank_hbm,
    last_ref, real_ref, imag_ref,
    vis, power_ref, square_ref, count_ref, mask_ref, high_ref, low_ref, twist_ref,
    flags, edge, smooth, recv, yhigh, ylow, send, spec, bank, held, done,
    load_sem, field_sem, table_sem, halo_send, halo_recv, send1, recv1, send2, recv2, done_sem,
):
    i, j = lax.axis_index("tm"), lax.axis_index("freq")
    x, zh, core, y, zl = place(i, j)
    barrier = pltpu.get_barrier_semaphore()

    for k in range(1, TM):
        pl.semaphore_signal(barrier, inc=1, device_id=(lax.rem(i + k, TM), j), device_id_type=MESH)
    for k in range(1, FREQ):
        pl.semaphore_signal(barrier, inc=1, device_id=(i, lax.rem(j + k, FREQ)), device_id_type=MESH)
    fields = [
        pltpu.make_async_copy(source, target, field_sem.at[n])
        for n, (source, target) in enumerate((
            (count_hbm, count_ref), (power_hbm, power_ref), (square_hbm, square_ref), (mask_hbm, mask_ref)))
    ]
    for copy in fields:
        copy.start()
    load = pltpu.make_async_copy(vis_hbm, vis, load_sem.at[0])
    load.start()

    tables = [
        pltpu.make_async_copy(source, target, table_sem.at[n])
        for n, (source, target) in enumerate(((high_hbm, high_ref), (low_hbm, low_ref), (twist_hbm, twist_ref)))
    ]
    for copy in tables:
        copy.start()
    for copy in fields:
        copy.wait()
    counts = count_ref[...].astype(F32)
    power = power_ref[...]
    kurtosis = (counts + 1.0) / (counts - 1.0) * (counts * square_ref[...] / (power * power) - 1.0)
    flags[...] = mask_ref[...].astype(F32) * jnp.exp(-2.0 * (kurtosis - 1.0) ** 2)

    pl.semaphore_wait(barrier, TM + FREQ - 2)
    right, left = lax.rem(i + 1, TM), lax.rem(i + TM - 1, TM)
    to_right = pltpu.make_async_remote_copy(
        flags.at[:, LEN - 128 : LEN], edge.at[0], halo_send.at[0], halo_recv.at[0],
        device_id=(right, j), device_id_type=MESH)
    to_left = pltpu.make_async_remote_copy(
        flags.at[:, 0:128], edge.at[1], halo_send.at[1], halo_recv.at[1],
        device_id=(left, j), device_id_type=MESH)
    to_right.start()
    to_left.start()
    blank = jnp.zeros((32, 128), F32)
    for rows in range(0, CHAN, 32):
        own = jnp.concatenate([blank, flags[rows : rows + 32, :], blank], axis=1)
        smooth[rows : rows + 32, :] = triangle(own)[:, 128 : 128 + LEN]
    to_right.wait()
    to_left.wait()
    lane = lax.broadcasted_iota(jnp.int32, (CHAN, 128), 1)
    first_lanes, last_lanes = lane < RIM, lane >= 128 - RIM
    before = triangle(jnp.where(last_lanes, edge[0], 0.0))
    after = triangle(jnp.where(first_lanes, edge[1], 0.0))
    smooth[:, 0:128] += jnp.where(first_lanes, before, 0.0)
    smooth[:, LEN - 128 : LEN] += jnp.where(last_lanes, after, 0.0)

    load.wait()
    bank_load = pltpu.make_async_copy(bank_hbm, bank, load_sem.at[1])
    bank_load.start()

    def first(e, o):
        d = tm_index(x, zh, core, o)
        dx, dzh, dcore, _, _ = place(d, j)
        return d, BLOCK * owner_block(dx, dcore, y, zl, e) + 2 * e + dzh

    def weigh(e, o):
        d, b = first(e, o)
        for c in range(2):
            value = (vis[c, b].astype(F32) * smooth[...]).astype(BF)
            if o == (0, 0, 0):
                recv[e, i, c] = value
            else:
                vis[c, b] = value

    def hand(e, o, c, rows):
        d, b = first(e, o)
        pltpu.make_async_remote_copy(
            vis.at[c, b, rows], recv.at[e, i, c, rows], send1.at[e], recv1.at[e],
            device_id=(d, j), device_id_type=MESH).start()

    size = CHAN // PIECES_1
    for e in range(2):
        order = shuffled(ORDER_1 + e)
        remote = [o for o in order if o != (0, 0, 0)]
        for o in order:
            weigh(e, o)
            if o != (0, 0, 0):
                hand(e, o, 0, pl.ds(0, size))
        def rest(q, _):
            rows = pl.ds(pl.multiple_of(q * size, size), size)
            for o in remote:
                hand(e, o, 0, rows)
            return 0
        lax.fori_loop(1, PIECES_1, rest, 0)
        def rest(q, _):
            rows = pl.ds(pl.multiple_of(q * size, size), size)
            for o in remote:
                hand(e, o, 1, rows)
            return 0
        lax.fori_loop(0, PIECES_1, rest, 0)

    for copy in tables:
        copy.wait()

    for e in range(2):
        others = recv.at[e, pl.ds(0, TM - 1)]
        pltpu.make_async_copy(others, others, recv1.at[e]).wait()

        def combine(step, _):
            rows = pl.ds(pl.multiple_of((step // 2) * 16, 16), 16)
            col = pl.multiple_of(lax.rem(step, 2) * 128, 128)
            cols = pl.ds(col, 128)
            inner = []
            for b in range(4):
                part = []
                for a in range(4):
                    p = 4 * a + b
                    part.append((recv[e, p, 0, rows, cols].astype(F32), recv[e, p, 1, rows, cols].astype(F32)))
                part = radix4(part)
                inner.append([cmul_w16(*part[c], b * c) for c in range(4)])
            for c in range(4):
                outer = radix4([inner[b][c] for b in range(4)])
                for d in range(4):
                    q = c + 4 * d
                    r, m = outer[d]
                    cosine = twist_ref[0, q : q + 1, cols]
                    sine = twist_ref[1, q : q + 1, cols]
                    for part, value in ((0, r * cosine + m * sine), (1, m * cosine - r * sine)):
                        top = value.astype(BF)
                        at = (q, rows, pl.ds(pl.multiple_of(col + LEN * part, 128), 128))
                        yhigh[at] = top
                        ylow[at] = (value - top.astype(F32)).astype(BF)
            return 0

        lax.fori_loop(0, 2 * CHAN // 16, combine, 0)

        dims = (((1,), (1,)), ((), ()))

        def transform(step, _):
            q = 2 * step
            yh = yhigh[pl.ds(q, 2)].reshape(2 * CHAN, 2 * LEN)
            yl = ylow[pl.ds(q, 2)].reshape(2 * CHAN, 2 * LEN)
            for part in range(2):
                rows = slice(LEN * part, LEN * part + LEN)
                value = lax.dot_general(high_ref[rows], yh, dims, preferred_element_type=F32)
                value += lax.dot_general(high_ref[rows], yl, dims, preferred_element_type=F32)
                value += lax.dot_general(low_ref[rows], yh, dims, preferred_element_type=F32)
                value = value.astype(BF)
                for h in range(2):
                    at = pl.ds(pl.multiple_of((q + h) * 16, 16), 16)
                    send[e, part, :, at, :] = value[:, CHAN * h : CHAN * h + CHAN].reshape(TM, TM, CHAN)
            return 0

        lax.fori_loop(0, TM // 2, transform, 0)

        dest = owner_block(x, core, y, zl, e)
        lanes = pl.ds(pl.multiple_of(j * CHAN, CHAN), CHAN)
        size2 = LEN // PIECES_2
        for c in range(2):
            part = 2 * e + c
            target = last_ref if part == 3 else spec.at[part]

            def share(q, _):
                rows = pl.ds(pl.multiple_of(q * size2, size2), size2)
                for o in shuffled(ORDER_2 + e):
                    d = tm_index(x, zh, core, o)

                    def away():
                        pltpu.make_async_remote_copy(
                            send.at[e, c, d, rows], target.at[zh, rows, lanes], send2, recv2.at[part],
                            device_id=(d, dest), device_id_type=MESH).start()

                    if o != (0, 0, 0):
                        away()
                    else:
                        pl.when(dest != j)(away)

                        @pl.when(dest == j)
                        def _():
                            pltpu.make_async_copy(
                                send.at[e, c, d, rows], target.at[zh, rows, lanes], recv2.at[part]).start()
                return 0

            lax.fori_loop(0, PIECES_2, share, 0)

    bank_load.wait()
    row_table = row_order()
    out = []
    for part in range(3):
        e, c = part // 2, part % 2
        pltpu.make_async_copy(spec.at[part], spec.at[part], recv2.at[part]).wait()
        for z in range(2):
            held[...] = jnp.dot(row_table, spec[part, z], preferred_element_type=F32).astype(BF)

            def rows_of(g, _):
                at = pl.ds(pl.multiple_of(g * 512, 512), 512)
                done[part, z, at, :] = lax.dot_general(
                    bank[class_ref[2 * e + z], at, :], held[...], (((1,), (1,)), ((), ())),
                    preferred_element_type=F32).astype(BF)
                return 0

            lax.fori_loop(0, 2, rows_of, 0)
        out.append(pltpu.make_async_copy(
            done.at[part], imag_ref if c else real_ref.at[pl.ds(2 * e, 2)], done_sem.at[part]))
        out[-1].start()

    pltpu.make_async_copy(last_ref, last_ref, recv2.at[3]).wait()
    for copy in out:
        copy.wait()
    for e in range(2):
        others = recv.at[e, pl.ds(0, TM - 1)]
        pltpu.make_async_copy(others, others, send1.at[e]).wait()
    own = jnp.logical_or(owner_block(x, core, y, zl, 0) == j, owner_block(x, core, y, zl, 1) == j)

    @pl.when(own)
    def _():
        most = vis.at[:, pl.ds(0, BLOCK * FREQ - 1)]
        pltpu.make_async_copy(most, most, send2).wait()

    @pl.when(jnp.logical_not(own))
    def _():
        pltpu.make_async_copy(vis, vis, send2).wait()


def exchange(classes, vis, power, square, count, mask, bank):
    high, low, twist = dft_tables()
    hbm, anywhere = pl.BlockSpec(memory_space=pltpu.HBM), pl.BlockSpec(memory_space=pl.ANY)
    dma = pltpu.SemaphoreType.DMA
    width = FREQ * CHAN
    return pl.pallas_call(
        exchange_kernel,
        name="exchange",
        out_shape=(
            jax.ShapeDtypeStruct((2, LEN, width), BF),
            jax.ShapeDtypeStruct((BLOCK, width, LEN), BF),
            jax.ShapeDtypeStruct((2, width, LEN), BF),
        ),
        in_specs=[pl.BlockSpec(memory_space=pltpu.SMEM)] + [hbm] * 9,
        out_specs=(anywhere, anywhere, anywhere),
        scratch_shapes=[
            pltpu.VMEM((2, BLOCK * FREQ, CHAN, LEN), BF),
            pltpu.VMEM((CHAN, LEN), F32),
            pltpu.VMEM((CHAN, LEN), F32),
            pltpu.VMEM((CHAN, LEN), jnp.int32),
            pltpu.VMEM((CHAN, LEN), jnp.int32),
            pltpu.VMEM((2 * LEN, 2 * LEN), BF),
            pltpu.VMEM((2 * LEN, 2 * LEN), BF),
            pltpu.VMEM((2, TM, LEN), F32),
            pltpu.VMEM((CHAN, LEN), F32),
            pltpu.VMEM((2, CHAN, 128), F32),
            pltpu.VMEM((CHAN, LEN), F32),
            pltpu.VMEM((2, TM, 2, CHAN, LEN), BF),
            pltpu.VMEM((TM, CHAN, 2 * LEN), BF),
            pltpu.VMEM((TM, CHAN, 2 * LEN), BF),
            pltpu.VMEM((2, 2, TM, LEN, CHAN), BF),
            pltpu.VMEM((3, 2, LEN, width), BF),
            pltpu.VMEM((4, width, width), BF),
            pltpu.VMEM((LEN, width), BF),
            pltpu.VMEM((3, 2, width, LEN), BF),
            dma((2,)), dma((4,)), dma((3,)), dma((2,)), dma((2,)), dma((2,)), dma((2,)), dma, dma((4,)), dma((3,)),
        ],
        compiler_params=pltpu.CompilerParams(
            collective_id=0, has_side_effects=True, vmem_limit_bytes=47 << 20),
    )(classes, *(pltpu.with_memory_space_constraint(value, pltpu.HBM) for value in (
        vis, power, square, count, mask, jnp.asarray(high), jnp.asarray(low), jnp.asarray(twist), bank)))


def finish_kernel(class_ref, last_ref, bank_ref, real_ref, imag_ref, out_ref, held, done, copy_sem, done_sem):
    copies = []
    for n in range(BLOCK + 2):
        source = real_ref.at[n] if n < BLOCK else imag_ref.at[n - BLOCK]
        copies.append(pltpu.make_async_copy(source, out_ref.at[n // BLOCK, n % BLOCK], copy_sem.at[n]))
        copies[-1].start()
    row_table = row_order()
    for z in range(2):
        held[z] = jnp.dot(row_table, last_ref[z], preferred_element_type=F32).astype(BF)
    for z in range(2):
        for h in range(2):
            rows = pl.ds(512 * h, 512)
            done[z, rows, :] = lax.dot_general(
                bank_ref[class_ref[2 + z], rows, :], held[z], (((1,), (1,)), ((), ())),
                preferred_element_type=F32).astype(BF)
            copies.append(pltpu.make_async_copy(done.at[z, rows], out_ref.at[1, 2 + z, rows], done_sem.at[z, h]))
            copies[-1].start()
    for copy in copies:
        copy.wait()


def finish(classes, last, bank, real, imag):
    width = FREQ * CHAN
    vmem, hbm = pl.BlockSpec(memory_space=pltpu.VMEM), pl.BlockSpec(memory_space=pl.ANY)
    dma = pltpu.SemaphoreType.DMA
    return pl.pallas_call(
        finish_kernel,
        name="finish",
        out_shape=jax.ShapeDtypeStruct((2, BLOCK, width, LEN), BF),
        in_specs=[pl.BlockSpec(memory_space=pltpu.SMEM)] + [vmem] * 4,
        out_specs=hbm,
        scratch_shapes=[
            pltpu.VMEM((2, LEN, width), BF),
            pltpu.VMEM((2, width, LEN), BF),
            dma((BLOCK + 2,)), dma((2, 2)),
        ],
        compiler_params=pltpu.CompilerParams(vmem_limit_bytes=20 << 20),
    )(classes, last, bank, real, imag)


def shards(visibility, power, square, count, mask, classes, bank):
    classes = classes[:, 0]
    last, real, imag = exchange(classes, visibility, power, square, count, mask, bank)
    return finish(classes, last, bank, real, imag)


def solution(mesh):
    in_specs = (
        P(None, None, "freq", "tm"),
        P("freq", "tm"),
        P("freq", "tm"),
        P("freq", "tm"),
        P("freq", "tm"),
        P("freq", None),
        P(),
    )
    out_specs = P(None, "freq", None, "tm")
    return jax.shard_map(shards, mesh=mesh, in_specs=in_specs, out_specs=out_specs, check_vma=False)
```

```python
import functools
import math
import random

import jax
import jax.numpy as jnp
import numpy as np
from jax import lax
from jax.experimental import pallas as pl
from jax.experimental.pallas import tpu as pltpu
from jax.sharding import PartitionSpec as P

RIM = 16
MESH = pl.DeviceIdType.MESH
TM, FREQ = 16, 8
CHAN, LEN = 128, 256
SAMPLES = TM * LEN
BLOCK = 4
BF, F32 = jnp.bfloat16, jnp.float32
PIECES_1, PIECES_2 = 4, 8
ORDER_1, ORDER_2 = 30, 21
OFFSETS = [(a, b, c) for a in range(4) for b in range(2) for c in range(2)]


def shuffled(seed):
    order = list(OFFSETS)
    random.Random(seed).shuffle(order)
    return order


def dft_tables():
    k = np.arange(LEN)
    angle = 2.0 * np.pi / LEN * (k[:, None] * k[None, :] % LEN)
    c, s = np.cos(angle), np.sin(angle)
    full = np.block([[c, s], [-s, c]]).astype(np.float32)
    high = full.astype(jnp.bfloat16)
    low = (full - high.astype(np.float32)).astype(jnp.bfloat16)
    turn = 2.0 * np.pi / SAMPLES * (np.arange(TM)[:, None] * k[None, :])
    twist = np.stack([np.cos(turn), np.sin(turn)]) / math.sqrt(SAMPLES)
    return high, low, twist.astype(np.float32)


def row_order():
    m = lax.broadcasted_iota(jnp.int32, (LEN, LEN), 0)
    r = lax.broadcasted_iota(jnp.int32, (LEN, LEN), 1)
    return jnp.where(lax.rem(m, TM) * TM + m // TM == r, 1.0, 0.0).astype(BF)


def place(i, j):
    return i // 4, lax.rem(i // 2, 2), lax.rem(i, 2), j // 2, lax.rem(j, 2)


def tm_index(x, zh, core, o):
    return lax.rem(x + o[0], 4) * 4 + lax.rem(zh + o[1], 2) * 2 + lax.rem(core + o[2], 2)


def owner_block(x, core, y, zl, e):
    return lax.rem(y + 2 * core + lax.rem(e + x, 2), 4) * 2 + lax.rem(zl + x // 2, 2)


def cmul_w16(r, i, n):
    n %= 16
    if n == 0:
        return r, i
    if n == 4:
        return i, -r
    if n == 8:
        return -r, -i
    if n == 12:
        return -i, r
    if n == 2:
        h = math.sqrt(0.5)
        return (r + i) * h, (i - r) * h
    if n == 6:
        h = math.sqrt(0.5)
        return (i - r) * h, -(r + i) * h
    c, s = math.cos(2 * math.pi * n / 16), math.sin(2 * math.pi * n / 16)
    return r * c + i * s, i * c - r * s


def radix4(v):
    (ar, ai), (br, bi), (cr, ci), (dr, di) = v
    pr, pi = ar + cr, ai + ci
    qr, qi = ar - cr, ai - ci
    sr, si = br + dr, bi + di
    tr, ti = br - dr, bi - di
    return [(pr + sr, pi + si), (qr + ti, qi - tr), (pr - sr, pi - si), (qr - ti, qi + tr)]


def box(v, direction):
    width = v.shape[1]

    def shift(u, n):
        return pltpu.roll(u, n if direction else width - n, 1)

    total = v
    for n in (1, 2, 4, 8):
        total = total + shift(total, n)
    return total + shift(v, 16)


def triangle(v):
    return box(box(v, 0), 1) * (1.0 / (RIM + 1) ** 2)


def exchange_kernel(
    class_ref, vis_hbm, power_hbm, square_hbm, count_hbm, mask_hbm, high_hbm, low_hbm, twist_hbm, bank_hbm,
    last_ref, real_ref, imag_ref,
    vis, power_ref, square_ref, count_ref, mask_ref, high_ref, low_ref, twist_ref,
    flags, edge, smooth, recv, yhigh, ylow, send, spec, bank, held, done,
    load_sem, field_sem, table_sem, halo_send, halo_recv, send1, recv1, send2, recv2, done_sem,
):
    i, j = lax.axis_index("tm"), lax.axis_index("freq")
    x, zh, core, y, zl = place(i, j)
    barrier = pltpu.get_barrier_semaphore()

    for k in range(1, TM):
        pl.semaphore_signal(barrier, inc=1, device_id=(lax.rem(i + k, TM), j), device_id_type=MESH)
    for k in range(1, FREQ):
        pl.semaphore_signal(barrier, inc=1, device_id=(i, lax.rem(j + k, FREQ)), device_id_type=MESH)
    fields = [
        pltpu.make_async_copy(source, target, field_sem.at[n])
        for n, (source, target) in enumerate((
            (count_hbm, count_ref), (power_hbm, power_ref), (square_hbm, square_ref), (mask_hbm, mask_ref)))
    ]
    for copy in fields:
        copy.start()
    load = pltpu.make_async_copy(vis_hbm, vis, load_sem.at[0])
    load.start()

    tables = [
        pltpu.make_async_copy(source, target, table_sem.at[n])
        for n, (source, target) in enumerate(((high_hbm, high_ref), (low_hbm, low_ref), (twist_hbm, twist_ref)))
    ]
    for copy in tables:
        copy.start()
    for copy in fields:
        copy.wait()
    counts = count_ref[...].astype(F32)
    power = power_ref[...]
    kurtosis = (counts + 1.0) / (counts - 1.0) * (counts * square_ref[...] / (power * power) - 1.0)
    flags[...] = mask_ref[...].astype(F32) * jnp.exp(-2.0 * (kurtosis - 1.0) ** 2)

    pl.semaphore_wait(barrier, TM + FREQ - 2)
    right, left = lax.rem(i + 1, TM), lax.rem(i + TM - 1, TM)
    to_right = pltpu.make_async_remote_copy(
        flags.at[:, LEN - 128 : LEN], edge.at[0], halo_send.at[0], halo_recv.at[0],
        device_id=(right, j), device_id_type=MESH)
    to_left = pltpu.make_async_remote_copy(
        flags.at[:, 0:128], edge.at[1], halo_send.at[1], halo_recv.at[1],
        device_id=(left, j), device_id_type=MESH)
    to_right.start()
    to_left.start()
    blank = jnp.zeros((32, 128), F32)
    for rows in range(0, CHAN, 32):
        own = jnp.concatenate([blank, flags[rows : rows + 32, :], blank], axis=1)
        smooth[rows : rows + 32, :] = triangle(own)[:, 128 : 128 + LEN]
    to_right.wait()
    to_left.wait()
    lane = lax.broadcasted_iota(jnp.int32, (CHAN, 128), 1)
    first_lanes, last_lanes = lane < RIM, lane >= 128 - RIM
    before = triangle(jnp.where(last_lanes, edge[0], 0.0))
    after = triangle(jnp.where(first_lanes, edge[1], 0.0))
    smooth[:, 0:128] += jnp.where(first_lanes, before, 0.0)
    smooth[:, LEN - 128 : LEN] += jnp.where(last_lanes, after, 0.0)

    load.wait()
    bank_load = pltpu.make_async_copy(bank_hbm, bank, load_sem.at[1])
    bank_load.start()

    def first(e, o):
        d = tm_index(x, zh, core, o)
        dx, dzh, dcore, _, _ = place(d, j)
        return d, BLOCK * owner_block(dx, dcore, y, zl, e) + 2 * e + dzh

    def weigh(e, o):
        d, b = first(e, o)
        for c in range(2):
            value = (vis[c, b].astype(F32) * smooth[...]).astype(BF)
            if o == (0, 0, 0):
                recv[e, i, c] = value
            else:
                vis[c, b] = value

    def hand(e, o, c, rows):
        d, b = first(e, o)
        pltpu.make_async_remote_copy(
            vis.at[c, b, rows], recv.at[e, i, c, rows], send1.at[e], recv1.at[e],
            device_id=(d, j), device_id_type=MESH).start()

    size = CHAN // PIECES_1
    for e in range(2):
        order = shuffled(ORDER_1 + e)
        remote = [o for o in order if o != (0, 0, 0)]
        for o in order:
            weigh(e, o)
            if o != (0, 0, 0):
                hand(e, o, 0, pl.ds(0, size))
        def rest(q, _):
            rows = pl.ds(pl.multiple_of(q * size, size), size)
            for o in remote:
                hand(e, o, 0, rows)
            return 0
        lax.fori_loop(1, PIECES_1, rest, 0)
        def rest(q, _):
            rows = pl.ds(pl.multiple_of(q * size, size), size)
            for o in remote:
                hand(e, o, 1, rows)
            return 0
        lax.fori_loop(0, PIECES_1, rest, 0)

    for copy in tables:
        copy.wait()

    for e in range(2):
        others = recv.at[e, pl.ds(0, TM - 1)]
        pltpu.make_async_copy(others, others, recv1.at[e]).wait()

        def combine(step, _):
            rows = pl.ds(pl.multiple_of((step // 2) * 16, 16), 16)
            col = pl.multiple_of(lax.rem(step, 2) * 128, 128)
            cols = pl.ds(col, 128)
            inner = []
            for b in range(4):
                part = []
                for a in range(4):
                    p = 4 * a + b
                    part.append((recv[e, p, 0, rows, cols].astype(F32), recv[e, p, 1, rows, cols].astype(F32)))
                part = radix4(part)
                inner.append([cmul_w16(*part[c], b * c) for c in range(4)])
            for c in range(4):
                outer = radix4([inner[b][c] for b in range(4)])
                for d in range(4):
                    q = c + 4 * d
                    r, m = outer[d]
                    cosine = twist_ref[0, q : q + 1, cols]
                    sine = twist_ref[1, q : q + 1, cols]
                    for part, value in ((0, r * cosine + m * sine), (1, m * cosine - r * sine)):
                        top = value.astype(BF)
                        at = (q, rows, pl.ds(pl.multiple_of(col + LEN * part, 128), 128))
                        yhigh[at] = top
                        ylow[at] = (value - top.astype(F32)).astype(BF)
            return 0

        lax.fori_loop(0, 2 * CHAN // 16, combine, 0)

        dims = (((1,), (1,)), ((), ()))

        def transform(step, _):
            q = 2 * step
            yh = yhigh[pl.ds(q, 2)].reshape(2 * CHAN, 2 * LEN)
            yl = ylow[pl.ds(q, 2)].reshape(2 * CHAN, 2 * LEN)
            for part in range(2):
                rows = slice(LEN * part, LEN * part + LEN)
                value = lax.dot_general(high_ref[rows], yh, dims, preferred_element_type=F32)
                value += lax.dot_general(high_ref[rows], yl, dims, preferred_element_type=F32)
                value += lax.dot_general(low_ref[rows], yh, dims, preferred_element_type=F32)
                value = value.astype(BF)
                for h in range(2):
                    at = pl.ds(pl.multiple_of((q + h) * 16, 16), 16)
                    send[e, part, :, at, :] = value[:, CHAN * h : CHAN * h + CHAN].reshape(TM, TM, CHAN)
            return 0

        lax.fori_loop(0, TM // 2, transform, 0)

        dest = owner_block(x, core, y, zl, e)
        lanes = pl.ds(pl.multiple_of(j * CHAN, CHAN), CHAN)
        size2 = LEN // PIECES_2
        for c in range(2):
            part = 2 * e + c
            target = last_ref if part == 3 else spec.at[part]

            def share(q, _):
                rows = pl.ds(pl.multiple_of(q * size2, size2), size2)
                for o in shuffled(ORDER_2 + e):
                    d = tm_index(x, zh, core, o)

                    def away():
                        pltpu.make_async_remote_copy(
                            send.at[e, c, d, rows], target.at[zh, rows, lanes], send2, recv2.at[part],
                            device_id=(d, dest), device_id_type=MESH).start()

                    if o != (0, 0, 0):
                        away()
                    else:
                        pl.when(dest != j)(away)

                        @pl.when(dest == j)
                        def _():
                            pltpu.make_async_copy(
                                send.at[e, c, d, rows], target.at[zh, rows, lanes], recv2.at[part]).start()
                return 0

            lax.fori_loop(0, PIECES_2, share, 0)

    bank_load.wait()
    row_table = row_order()
    out = []
    for part in range(3):
        e, c = part // 2, part % 2
        pltpu.make_async_copy(spec.at[part], spec.at[part], recv2.at[part]).wait()
        for z in range(2):
            held[...] = jnp.dot(row_table, spec[part, z], preferred_element_type=F32).astype(BF)

            def rows_of(g, _):
                at = pl.ds(pl.multiple_of(g * 512, 512), 512)
                done[part, z, at, :] = lax.dot_general(
                    bank[class_ref[2 * e + z], at, :], held[...], (((1,), (1,)), ((), ())),
                    preferred_element_type=F32).astype(BF)
                return 0

            lax.fori_loop(0, 2, rows_of, 0)
        out.append(pltpu.make_async_copy(
            done.at[part], imag_ref if c else real_ref.at[pl.ds(2 * e, 2)], done_sem.at[part]))
        out[-1].start()

    pltpu.make_async_copy(last_ref, last_ref, recv2.at[3]).wait()
    for copy in out:
        copy.wait()
    for e in range(2):
        others = recv.at[e, pl.ds(0, TM - 1)]
        pltpu.make_async_copy(others, others, send1.at[e]).wait()
    own = jnp.logical_or(owner_block(x, core, y, zl, 0) == j, owner_block(x, core, y, zl, 1) == j)

    @pl.when(own)
    def _():
        most = vis.at[:, pl.ds(0, BLOCK * FREQ - 1)]
        pltpu.make_async_copy(most, most, send2).wait()

    @pl.when(jnp.logical_not(own))
    def _():
        pltpu.make_async_copy(vis, vis, send2).wait()


def exchange(classes, vis, power, square, count, mask, bank):
    high, low, twist = dft_tables()
    hbm, anywhere = pl.BlockSpec(memory_space=pltpu.HBM), pl.BlockSpec(memory_space=pl.ANY)
    dma = pltpu.SemaphoreType.DMA
    width = FREQ * CHAN
    return pl.pallas_call(
        exchange_kernel,
        name="exchange",
        out_shape=(
            jax.ShapeDtypeStruct((2, LEN, width), BF),
            jax.ShapeDtypeStruct((BLOCK, width, LEN), BF),
            jax.ShapeDtypeStruct((2, width, LEN), BF),
        ),
        in_specs=[pl.BlockSpec(memory_space=pltpu.SMEM)] + [hbm] * 9,
        out_specs=(anywhere, anywhere, anywhere),
        scratch_shapes=[
            pltpu.VMEM((2, BLOCK * FREQ, CHAN, LEN), BF),
            pltpu.VMEM((CHAN, LEN), F32),
            pltpu.VMEM((CHAN, LEN), F32),
            pltpu.VMEM((CHAN, LEN), jnp.int32),
            pltpu.VMEM((CHAN, LEN), jnp.int32),
            pltpu.VMEM((2 * LEN, 2 * LEN), BF),
            pltpu.VMEM((2 * LEN, 2 * LEN), BF),
            pltpu.VMEM((2, TM, LEN), F32),
            pltpu.VMEM((CHAN, LEN), F32),
            pltpu.VMEM((2, CHAN, 128), F32),
            pltpu.VMEM((CHAN, LEN), F32),
            pltpu.VMEM((2, TM, 2, CHAN, LEN), BF),
            pltpu.VMEM((TM, CHAN, 2 * LEN), BF),
            pltpu.VMEM((TM, CHAN, 2 * LEN), BF),
            pltpu.VMEM((2, 2, TM, LEN, CHAN), BF),
            pltpu.VMEM((3, 2, LEN, width), BF),
            pltpu.VMEM((4, width, width), BF),
            pltpu.VMEM((LEN, width), BF),
            pltpu.VMEM((3, 2, width, LEN), BF),
            dma((2,)), dma((4,)), dma((3,)), dma((2,)), dma((2,)), dma((2,)), dma((2,)), dma, dma((4,)), dma((3,)),
        ],
        compiler_params=pltpu.CompilerParams(
            collective_id=0, has_side_effects=True, vmem_limit_bytes=47 << 20),
    )(classes, *(pltpu.with_memory_space_constraint(value, pltpu.HBM) for value in (
        vis, power, square, count, mask, jnp.asarray(high), jnp.asarray(low), jnp.asarray(twist), bank)))


def finish_kernel(class_ref, last_ref, bank_ref, real_ref, imag_ref, out_ref, held, done, copy_sem, done_sem):
    copies = []
    for n in range(BLOCK + 2):
        source = real_ref.at[n] if n < BLOCK else imag_ref.at[n - BLOCK]
        copies.append(pltpu.make_async_copy(source, out_ref.at[n // BLOCK, n % BLOCK], copy_sem.at[n]))
        copies[-1].start()
    row_table = row_order()
    for z in range(2):
        held[z] = jnp.dot(row_table, last_ref[z], preferred_element_type=F32).astype(BF)
    for z in range(2):
        for h in range(2):
            rows = pl.ds(512 * h, 512)
            done[z, rows, :] = lax.dot_general(
                bank_ref[class_ref[2 + z], rows, :], held[z], (((1,), (1,)), ((), ())),
                preferred_element_type=F32).astype(BF)
            copies.append(pltpu.make_async_copy(done.at[z, rows], out_ref.at[1, 2 + z, rows], done_sem.at[z, h]))
            copies[-1].start()
    for copy in copies:
        copy.wait()


def finish(classes, last, bank, real, imag):
    width = FREQ * CHAN
    vmem, hbm = pl.BlockSpec(memory_space=pltpu.VMEM), pl.BlockSpec(memory_space=pl.ANY)
    dma = pltpu.SemaphoreType.DMA
    return pl.pallas_call(
        finish_kernel,
        name="finish",
        out_shape=jax.ShapeDtypeStruct((2, BLOCK, width, LEN), BF),
        in_specs=[pl.BlockSpec(memory_space=pltpu.SMEM)] + [vmem] * 4,
        out_specs=hbm,
        scratch_shapes=[
            pltpu.VMEM((2, LEN, width), BF),
            pltpu.VMEM((2, width, LEN), BF),
            dma((BLOCK + 2,)), dma((2, 2)),
        ],
        compiler_params=pltpu.CompilerParams(vmem_limit_bytes=20 << 20),
    )(classes, last, bank, real, imag)


def shards(visibility, power, square, count, mask, classes, bank):
    classes = classes[:, 0]
    last, real, imag = exchange(classes, visibility, power, square, count, mask, bank)
    return finish(classes, last, bank, real, imag)


def solution(mesh):
    in_specs = (
        P(None, None, "freq", "tm"),
        P("freq", "tm"),
        P("freq", "tm"),
        P("freq", "tm"),
        P("freq", "tm"),
        P("freq", None),
        P(),
    )
    out_specs = P(None, "freq", None, "tm")
    return jax.shard_map(shards, mesh=mesh, in_specs=in_specs, out_specs=out_specs, check_vma=False)
```
